32 devices in a mesh: ep: 16 (over z, y, x), dp: 2 (over core).
Axes of the slice: x: 2, y: 2, z: 4, core: 2. Of those that a mesh axis runs over, the one named last changes fastest.
Arguments:
- tokens: bfloat16 [4096, 2048], P(('ep', 'dp')), may hold values from -6 to 6
- grad_out: bfloat16 [4096, 2048], P(('ep', 'dp')), may hold values from -6 to 6
- expert_ids: int32 [4096, 8], P(('ep', 'dp')), may hold values from 0 to 15, all different within a row; in each aligned block of 128 rows (0 to 127, 128 to 255, ...) at most 72 rows name the same one
- route_weight: bfloat16 [4096, 8], P(('ep', 'dp')), may hold values from 0.019897461 to 0.25
- experts: bfloat16 [16, 3, 2048, 384], P('ep'), may hold values from -0.125 to 0.125
- error_in: bfloat16 [16, 3, 2048, 384], P('ep', None, 'dp'), may hold values from -0.29882812 to 0.29882812
- hot_expert: int32 [1], replicated, may hold values from 0 to 15
- keep_rows: int32 [128], replicated, may hold values from 0 to 2047, as said below
Outputs:
- d_tokens: bfloat16 [4096, 2048], P(('ep', 'dp'))
- d_route: bfloat16 [4096, 8], P(('ep', 'dp'))
- d_experts: bfloat16 [16, 3, 2048, 384], P('ep', None, 'dp')
- error_out: bfloat16 [16, 3, 2048, 384], P('ep', None, 'dp')
The draws below stay inside these ranges and needn't reach their ends.
Inputs may be any that keep to these rules, and one draw needn't show every extreme that they name: `expert_ids`: each token names 8 different experts; at most 72 tokens of one device name one expert, and that bound is reached. `keep_rows`: 128 distinct rows.
All inputs are finite; a program needn't handle non-finite values.
Results may differ from the reference program's by a relative error of at most 0.012.
Values may be sent and summed in bfloat16 or wider, within the bound.
No kernel may reach another device: no remote copies, remote signals or barrier semaphores. Data moves between devices by JAX's collectives and lax.ppermute only.
A program may use at most 192 MiB of HBM per device.

```python
import math
import jax
import jax.numpy as jnp
import numpy as np
from jax import lax

D = 2048
FF = 384
TOP = 8
TOK_DEV = 128
EXPERTS = 16
CAP = 72
KEEP = 128
TOKENS = 4096
N_EP = 16
N_DP = 2


def draw_keep_rows(key, part):
    return jax.random.permutation(key, D)[:KEEP].astype(jnp.int32)


def block_levels(key, extent, split, smallest, largest):
    def one(position, shards_of):
        steps = jax.random.uniform(jax.random.fold_in(jax.random.fold_in(key, 6), position), (shards_of,), jnp.float32, smallest / len(split), largest / len(split))
        return jnp.repeat(jnp.exp(steps), extent[position] // shards_of).reshape((-1,) + (1,) * (len(extent) - position - 1))

    loudness = one(*split[0])
    for cut in split[1:]:
        loudness = loudness * one(*cut)
    return loudness


def assign_block(key, own, number, rows, count, top, most, lean):
    sequence = jax.random.permutation(key, count)
    crowded, ordinary = portions_of(count, rows * top, most, lean, True), portions_of(count, rows * top, most, lean, False)
    places = jnp.arange(count)

    def named(sizes, offset_by):
        used = int((sizes > 0).sum())
        fixed = max(1, used // 4)
        moved = fixed + (places - fixed + offset_by * (used - fixed)) % max(1, count - fixed)
        return jnp.zeros((count,), jnp.int32).at[sequence[jnp.where(places < fixed, places, moved)]].set(jnp.asarray(sizes, jnp.int32))

    sizes = jnp.where(number % 4 == 0, named(crowded, number // 4), named(ordinary, number - number // 4 - 1))
    mixed = jax.random.permutation(jax.random.fold_in(own, 3), count)
    donor, sink = mixed[0:count // 2 * 2:2], mixed[1:count // 2 * 2:2]
    slack = jnp.minimum(sizes[donor] - 1, most - sizes[sink]) // 2
    slack = jnp.where((donor == sequence[0]) | (sink == sequence[0]) | (sizes[sink] == 0), 0, jnp.maximum(slack, 0))
    moved = jax.random.randint(jax.random.fold_in(own, 4), (count // 2,), 0, 1 << 20) % (slack + 1)
    sizes = sizes.at[donor].add(-moved).at[sink].add(moved)
    items = jnp.searchsorted(jnp.cumsum(sizes), jnp.arange(rows * top), side="right").astype(jnp.int32)
    table = items.reshape(top, rows).T
    table = table[jax.random.permutation(jax.random.fold_in(own, 1), rows)]
    offset_by = jax.random.randint(jax.random.fold_in(own, 2), (rows, 1), 0, top)
    return jnp.take_along_axis(table, (jnp.arange(top)[None, :] + offset_by) % top, axis=1)


def portions_of(count, total, bound, slope, full):
    loads = [(1 << 20) // math.isqrt(standing ** slope) + 1 for standing in range(1, count + 1)]
    largest = bound if full else min(bound, max(-(-total // count), total * loads[0] // sum(loads)))
    least = 1 if total - largest >= count - 1 else 0
    given, surplus = [largest] + [least] * (count - 1), total - largest - least * (count - 1)
    while surplus > 0:
        free = [i for i in range(1, count) if given[i] < largest] or [i for i in range(1, count) if given[i] < bound]
        whole, budget = sum([loads[i] for i in free]), surplus
        for i in free:
            extra = min(bound - given[i], max(1, budget * loads[i] // whole), surplus)
            given[i] = given[i] + extra
            surplus = surplus - extra
    return np.array(given)


def scatter_about(key, dims, scale, bound, shards=(), held_as=jnp.bfloat16):
    drawn = scale * jax.random.normal(key, dims, jnp.float32)
    if shards:
        drawn = drawn * block_levels(key, dims, shards, -0.22, 0.18)
    return jnp.clip(drawn, -bound, bound).astype(held_as)


def setup_inputs(seed: int = 0) -> dict:
    streams_of = jax.random.split(jax.random.key(seed), 9)
    tokens = scatter_about(streams_of[0], (TOKENS, D), 1.0, 6.0, ((0, 32),))
    grad_out = scatter_about(streams_of[1], (TOKENS, D), 1.0, 6.0, ((0, 32),))
    expert_ids_keys = jax.random.split(jax.random.fold_in(streams_of[2], 1), TOKENS // TOK_DEV)
    expert_ids_turns = jax.random.permutation(jax.random.fold_in(streams_of[2], 3), TOKENS // TOK_DEV)
    expert_ids = jax.vmap(lambda own, number: assign_block(jax.random.fold_in(streams_of[2], 2), own, number, TOK_DEV, EXPERTS, TOP, CAP, 1))(expert_ids_keys, expert_ids_turns).reshape((TOKENS, TOP))
    route_weight = jnp.clip(0.019897461 + 0.23010254 * jax.random.uniform(streams_of[3], (TOKENS, TOP), jnp.float32) ** block_levels(streams_of[3], (TOKENS, TOP), ((0, 32),), -0.2, 0.2), 0.019897461, 0.25).astype(jnp.bfloat16)
    experts = scatter_about(streams_of[4], (EXPERTS, 3, D, FF), D ** -0.5, 0.125, ((0, 16),))
    error_in = scatter_about(streams_of[5], (N_EP, 3, D, FF), 0.05, 0.29882812, ((0, 16), (2, 2)))
    hot_expert = jax.random.randint(streams_of[6], (1,), 0, EXPERTS).astype(jnp.int32)
    keep_rows = draw_keep_rows(jax.random.fold_in(streams_of[8], 71), 0)
    return dict(tokens=tokens, grad_out=grad_out, expert_ids=expert_ids, route_weight=route_weight, experts=experts, error_in=error_in, hot_expert=hot_expert, keep_rows=keep_rows)


def expert_rows(rows_x, rows_dy, rows_p, weights):
    gate_pre = jnp.dot(rows_x, weights[0], preferred_element_type=jnp.float32)
    up_pre = jnp.dot(rows_x, weights[1], preferred_element_type=jnp.float32)
    back_proj = jnp.dot(rows_dy, weights[2], preferred_element_type=jnp.float32)
    sigmoid_g = jax.nn.sigmoid(gate_pre)
    silu_g = gate_pre * sigmoid_g
    active = silu_g * up_pre
    d_score = jnp.sum(active * back_proj, axis=1).astype(jnp.bfloat16)
    scale_p = rows_p.astype(jnp.float32)[:, None]
    grad_h = scale_p * back_proj
    d_gate = (grad_h * up_pre * sigmoid_g * (1.0 + gate_pre * (1.0 - sigmoid_g))).astype(jnp.bfloat16)
    d_up = (grad_h * silu_g).astype(jnp.bfloat16)
    hidden_w = (scale_p * active).astype(jnp.bfloat16)
    grad_x = (jnp.dot(d_gate, weights[0].T, preferred_element_type=jnp.float32)
              + jnp.dot(d_up, weights[1].T, preferred_element_type=jnp.float32)).astype(jnp.bfloat16)
    grads = jnp.stack([
        jnp.dot(rows_x.T, d_gate, preferred_element_type=jnp.float32),
        jnp.dot(rows_x.T, d_up, preferred_element_type=jnp.float32),
        jnp.dot(rows_dy.T, hidden_w, preferred_element_type=jnp.float32)])
    return grad_x, d_score, grads


def rounded(values):
    return lax.optimization_barrier(values.astype(jnp.bfloat16)).astype(jnp.float32)


def reference(tokens, grad_out, expert_ids, route_weight, experts, error_in, hot_expert, keep_rows):
    blocks = N_EP * N_DP
    assigns = TOK_DEV * TOP
    id_blocks = expert_ids.reshape(blocks, assigns)
    onehot = (id_blocks[:, :, None] == jnp.arange(EXPERTS, dtype=jnp.int32)[None, None, :]).astype(jnp.int32)
    ranks = jnp.sum(jnp.cumsum(onehot, axis=1) * onehot, axis=2) - 1
    x_blocks = tokens.reshape(blocks, TOK_DEV, D)
    dy_blocks = grad_out.reshape(blocks, TOK_DEV, D)
    p_blocks = route_weight.reshape(blocks, assigns)
    hot_id = hot_expert[0]
    block_ids = jnp.arange(blocks, dtype=jnp.int32)[:, None]

    def slots_for(expert):
        matched = (id_blocks == expert)[:, :, None] & (ranks[:, :, None] == jnp.arange(CAP, dtype=jnp.int32)[None, None, :])
        picked = jnp.sum(jnp.where(matched, (jnp.arange(assigns, dtype=jnp.int32) + 1)[None, :, None], 0), axis=1) - 1
        filled = picked >= 0
        safe_idx = jnp.maximum(picked, 0).astype(jnp.int32)
        tok_idx = (safe_idx // TOP).astype(jnp.int32)
        slot_x = jnp.where(filled[..., None], jnp.take_along_axis(x_blocks, tok_idx[..., None], axis=1), 0).astype(jnp.bfloat16)
        slot_dy = jnp.where(filled[..., None], jnp.take_along_axis(dy_blocks, tok_idx[..., None], axis=1), 0).astype(jnp.bfloat16)
        slot_p = jnp.where(filled, jnp.take_along_axis(p_blocks, safe_idx, axis=1), 0).astype(jnp.bfloat16)
        return slot_x, slot_dy, slot_p, filled, safe_idx, tok_idx

    def cold_step(carry, expert):
        dx_sum, route_sum = carry
        slot_x, slot_dy, slot_p, filled, safe_idx, tok_idx = slots_for(expert)
        weights = experts[expert]
        grouped_x = slot_x.reshape(N_EP, N_DP, CAP, D)
        grouped_dy = slot_dy.reshape(N_EP, N_DP, CAP, D)
        grouped_p = slot_p.reshape(N_EP, N_DP, CAP)
        dx_parts = []
        score_parts = []
        summed = jnp.zeros((3, D, FF), jnp.float32)
        for group in range(N_DP):
            grad_x, d_score, grads = expert_rows(grouped_x[:, group].reshape(N_EP * CAP, D),
                                                 grouped_dy[:, group].reshape(N_EP * CAP, D),
                                                 grouped_p[:, group].reshape(N_EP * CAP), weights)
            dx_parts.append(grad_x.reshape(N_EP, CAP, D))
            score_parts.append(d_score.reshape(N_EP, CAP))
            summed = summed + rounded(grads)
        grad_x = jnp.stack(dx_parts, axis=1).reshape(blocks, CAP, D)
        d_score = jnp.stack(score_parts, axis=1).reshape(blocks, CAP)
        is_cold = (expert != hot_id).astype(jnp.float32)
        grads_out = (summed * is_cold).astype(jnp.bfloat16)
        dx_sum = dx_sum.at[block_ids, tok_idx].add(jnp.where(filled[..., None], grad_x.astype(jnp.float32), 0.0))
        route_sum = route_sum.at[block_ids, safe_idx].add(jnp.where(filled, d_score.astype(jnp.float32), 0.0))
        return (dx_sum, route_sum), grads_out

    start_carry = (jnp.zeros((blocks, TOK_DEV, D), jnp.float32), jnp.zeros((blocks, assigns), jnp.float32))
    (dx_sum, route_sum), cold_grads = lax.scan(cold_step, start_carry, jnp.arange(EXPERTS, dtype=jnp.int32))

    hot_x, hot_dy, hot_p, hot_filled, hot_safe, hot_tok = slots_for(hot_id)
    hot_weights = experts[hot_id]

    def per_chip(chip):
        summed = jnp.zeros((3, D, FF), jnp.float32)
        for group in range(N_DP):
            block = chip * N_DP + group
            grad_x, d_score, grads = expert_rows(hot_x[block], hot_dy[block], hot_p[block], hot_weights)
            summed = summed + rounded(grads)
        accum = summed + error_in[chip].astype(jnp.float32)
        chosen = accum[:, keep_rows, :]
        remain = accum.at[:, keep_rows, :].set(0.0).astype(jnp.bfloat16)
        return chosen, remain

    chosen_all, error_out = lax.map(per_chip, jnp.arange(N_EP, dtype=jnp.int32))
    kept = jnp.sum(chosen_all, axis=0)
    hot_grad = jnp.zeros((3, D, FF), jnp.float32).at[:, keep_rows, :].set(kept).astype(jnp.bfloat16)
    d_experts = lax.dynamic_update_index_in_dim(cold_grads, hot_grad, hot_id, 0)
    d_tokens = dx_sum.reshape(TOKENS, D).astype(jnp.bfloat16)
    d_route = route_sum.reshape(TOKENS, TOP).astype(jnp.bfloat16)
    return d_tokens, d_route, d_experts, error_out
```

```python
import functools
import jax
import jax.numpy as jnp
from jax import lax
from jax.experimental import pallas as pl
from jax.experimental.pallas import tpu as pltpu
from jax.sharding import PartitionSpec as P


def spread(x, axis, root):
    mine = lax.axis_index(axis) == root
    return lax.psum(jnp.where(mine, x, jnp.zeros_like(x)), axis)


def expert_rows(rows_x, rows_dy, rows_p, weights):
    gate_pre = jnp.dot(rows_x, weights[0], preferred_element_type=jnp.float32)
    up_pre = jnp.dot(rows_x, weights[1], preferred_element_type=jnp.float32)
    back_proj = jnp.dot(rows_dy, weights[2], preferred_element_type=jnp.float32)
    sigmoid_g = jax.nn.sigmoid(gate_pre)
    silu_g = gate_pre * sigmoid_g
    active = silu_g * up_pre
    d_score = jnp.sum(active * back_proj, axis=1).astype(jnp.bfloat16)
    scale_p = rows_p.astype(jnp.float32)[:, None]
    grad_h = scale_p * back_proj
    d_gate = (grad_h * up_pre * sigmoid_g * (1.0 + gate_pre * (1.0 - sigmoid_g))).astype(
        jnp.bfloat16
    )
    d_up = (grad_h * silu_g).astype(jnp.bfloat16)
    hidden_w = (scale_p * active).astype(jnp.bfloat16)
    contract = (((1,), (1,)), ((), ()))
    grad_x = (
        lax.dot_general(d_gate, weights[0], contract, preferred_element_type=jnp.float32)
        + lax.dot_general(d_up, weights[1], contract, preferred_element_type=jnp.float32)
    ).astype(jnp.bfloat16)
    outer = (((0,), (0,)), ((), ()))
    grads = jnp.stack(
        [
            lax.dot_general(rows_x, d_gate, outer, preferred_element_type=jnp.float32),
            lax.dot_general(rows_x, d_up, outer, preferred_element_type=jnp.float32),
            lax.dot_general(rows_dy, hidden_w, outer, preferred_element_type=jnp.float32),
        ]
    )
    return (grad_x, d_score, grads)


def sparse_body(tokens, grad_out, expert_ids, route_weight, experts, error_in, hot_expert, keep_rows):
    n_owners = lax.axis_size("ep")
    n_cores = lax.axis_size("dp")
    tok_count, top_count = expert_ids.shape
    width = tokens.shape[1]
    assigns = tok_count * top_count
    capacity = 9 * assigns // (8 * n_owners)
    slot_rows = n_owners * capacity
    half_rows = width // n_cores
    row_start = lax.axis_index("dp") * half_rows
    hot_id = hot_expert[0]
    flat_ids = expert_ids.reshape(assigns)
    position = jnp.arange(assigns, dtype=jnp.int32)
    onehot = (flat_ids[:, None] == jnp.arange(n_owners, dtype=jnp.int32)[None, :]).astype(
        jnp.bfloat16
    )
    earlier = (position[:, None] > position[None, :]).astype(jnp.bfloat16)
    before = jnp.dot(earlier, onehot, preferred_element_type=jnp.float32)
    ranks = jnp.sum(before * onehot.astype(jnp.float32), axis=1).astype(jnp.int32)
    slot_of = flat_ids * capacity + ranks
    source = jnp.full((slot_rows,), -1, jnp.int32).at[slot_of].set(position)
    filled = source >= 0
    safe_idx = jnp.maximum(source, 0)
    owner_row = jnp.arange(slot_rows, dtype=jnp.int32) // capacity
    cold_slot = filled & (owner_row != hot_id)
    slot_x = jnp.where(filled[:, None], jnp.take(tokens, safe_idx // top_count, axis=0), 0)
    slot_dy = jnp.where(filled[:, None], jnp.take(grad_out, safe_idx // top_count, axis=0), 0)
    slot_p = jnp.where(filled, jnp.take(route_weight.reshape(assigns), safe_idx), 0)
    send_x = jnp.where(cold_slot[:, None], slot_x, 0).reshape(n_owners, capacity, width)
    send_dy = jnp.where(cold_slot[:, None], slot_dy, 0).reshape(n_owners, capacity, width)
    send_p = jnp.where(cold_slot, slot_p, 0).reshape(n_owners, capacity)
    recv_x, recv_dy, recv_p = (
        lax.all_to_all(send_x, "ep", split_axis=0, concat_axis=0, tiled=True),
        lax.all_to_all(send_dy, "ep", split_axis=0, concat_axis=0, tiled=True),
        lax.all_to_all(send_p, "ep", split_axis=0, concat_axis=0, tiled=True),
    )
    owned = experts[0]
    my_rows = lax.dynamic_slice_in_dim(owned, row_start, half_rows, 1)
    hot_rows = spread(my_rows, "ep", hot_id)
    hot_weights = lax.all_gather(hot_rows, "dp", axis=1, tiled=True)
    cold_dx, cold_score, cold_grads = expert_rows(
        recv_x.reshape(slot_rows, width),
        recv_dy.reshape(slot_rows, width),
        recv_p.reshape(slot_rows),
        owned,
    )
    back_dx, back_score = (
        lax.all_to_all(
            cold_dx.reshape(n_owners, capacity, width),
            "ep",
            split_axis=0,
            concat_axis=0,
            tiled=True,
        ),
        lax.all_to_all(
            cold_score.reshape(n_owners, capacity), "ep", split_axis=0, concat_axis=0, tiled=True
        ),
    )
    hot_x = lax.dynamic_slice_in_dim(slot_x, hot_id * capacity, capacity, 0)
    hot_dy = lax.dynamic_slice_in_dim(slot_dy, hot_id * capacity, capacity, 0)
    hot_p = lax.dynamic_slice_in_dim(slot_p, hot_id * capacity, capacity, 0)
    hot_dx, hot_score, hot_grads = expert_rows(hot_x, hot_dy, hot_p, hot_weights)
    all_dx = lax.dynamic_update_slice_in_dim(
        back_dx.reshape(slot_rows, width), hot_dx, hot_id * capacity, 0
    )
    all_score = lax.dynamic_update_slice_in_dim(
        back_score.reshape(slot_rows), hot_score, hot_id * capacity, 0
    )
    d_tokens = jnp.sum(
        jnp.take(all_dx, slot_of, axis=0).astype(jnp.float32).reshape(tok_count, top_count, width),
        axis=1,
    ).astype(jnp.bfloat16)
    d_route = jnp.take(all_score, slot_of).reshape(tok_count, top_count)
    cold_sum, shadow_sum = (
        lax.psum_scatter(
            cold_grads.astype(jnp.bfloat16), "dp", scatter_dimension=1, tiled=True
        ).astype(jnp.float32),
        lax.psum_scatter(
            hot_grads.astype(jnp.bfloat16), "dp", scatter_dimension=1, tiled=True
        ).astype(jnp.float32),
    )
    accum = shadow_sum + error_in[0].astype(jnp.float32)
    local_keep = keep_rows - row_start
    inside = (local_keep >= 0) & (local_keep < half_rows)
    clipped = jnp.clip(local_keep, 0, half_rows - 1)
    chosen = jnp.where(inside[None, :, None], jnp.take(accum, clipped, axis=1), 0.0)
    dropped = jnp.zeros((half_rows,), jnp.int32).at[clipped].add(inside.astype(jnp.int32)) > 0
    error_out = jnp.where(dropped[None, :, None], 0.0, accum).astype(jnp.bfloat16)[None]
    kept = lax.psum(chosen, "ep")
    unpacked = (
        jnp.zeros_like(accum).at[:, clipped, :].add(jnp.where(inside[None, :, None], kept, 0.0))
    )
    is_owner = lax.axis_index("ep") == hot_id
    d_experts = (cold_sum + jnp.where(is_owner, unpacked, 0.0)).astype(jnp.bfloat16)[None]
    return (d_tokens, d_route, d_experts, error_out)


LANES = 128
BF16 = jnp.bfloat16
F32 = jnp.float32
ROWS_T = (((0,), (0,)), ((), ()))
COLS_T = (((1,), (1,)), ((), ()))


def expert_kernel(ids_ref, *refs, count, width, hidden):
    msgs = refs[:count]
    weights = refs[count : count + 2]
    backs = refs[count + 2 : 2 * count + 2]
    dvals = refs[2 * count + 2 :]
    rows = msgs[0].shape[0]
    whole = lambda lo, hi: jnp.concatenate([m[:, lo:hi] for m in msgs], axis=0)
    x = whole(0, width)
    dy = whole(width, 2 * width)
    probs = whole(2 * width, msgs[0].shape[1]).astype(F32)
    lanes = probs.shape[1]
    lane = lax.broadcasted_iota(jnp.int32, probs.shape, 1)
    score = jnp.zeros(probs.shape, F32)
    hot = ids_ref[2]
    pair = []
    for n, w in enumerate(weights):
        mine = lane == ids_ref[n]
        p = jnp.sum(jnp.where(mine, probs, 0.0), axis=1, keepdims=True)
        gate = jnp.dot(x, w[0], preferred_element_type=F32)
        up = jnp.dot(x, w[1], preferred_element_type=F32)
        back = jnp.dot(dy, w[2], preferred_element_type=F32)
        sig = jax.nn.sigmoid(gate)
        silu = gate * sig
        act = silu * up
        score = jnp.where(mine, jnp.sum(act * back, axis=1, keepdims=True), score)
        grad_h = p * back
        d_gate = (grad_h * up * sig * (1.0 + gate * (1.0 - sig))).astype(BF16)
        d_up = (grad_h * silu).astype(BF16)
        hidden_w = (p * act).astype(BF16)
        pair.append((d_gate, d_up, hidden_w))
        for i in range(count):
            for k, d in enumerate((d_gate, d_up, hidden_w)):
                lo = (3 * n + k) * hidden
                dvals[i][:, lo : lo + hidden] = d[i * rows : (i + 1) * rows]
    hot_lo = width + lanes
    for i in range(count):
        backs[i][:, width:hot_lo] = score[i * rows : (i + 1) * rows].astype(BF16)

        @pl.when(jnp.logical_and(hot != ids_ref[0], hot != ids_ref[1]))
        def _():
            backs[i][:, hot_lo:] = jnp.zeros((rows, 3 * hidden), BF16)

        for n in range(2):

            @pl.when(hot == ids_ref[n])
            def _():
                backs[i][:, hot_lo:] = dvals[i][:, 3 * n * hidden : 3 * (n + 1) * hidden]

    d_all = jnp.concatenate([pair[0][0], pair[0][1], pair[1][0], pair[1][1]], axis=1)
    step = 2 * LANES
    for lo in range(0, width, step):
        part = jnp.concatenate([w[k, lo : lo + step, :] for w in weights for k in range(2)], axis=1)
        dx = lax.dot_general(d_all, part, COLS_T, preferred_element_type=F32).astype(BF16)
        for i in range(count):
            backs[i][:, lo : lo + step] = dx[i * rows : (i + 1) * rows]


def run_experts(ids, msgs, own, neighbour):
    count = len(msgs)
    rows, cols = msgs[0].shape
    _, width, hidden = own.shape
    lanes = cols - 2 * width
    vmem = pl.BlockSpec(memory_space=pltpu.VMEM)
    back = jax.ShapeDtypeStruct((rows, width + lanes + 3 * hidden), BF16)
    dval = jax.ShapeDtypeStruct((rows, 6 * hidden), BF16)
    flops = 20 * count * rows * width * hidden
    out = pl.pallas_call(
        functools.partial(expert_kernel, count=count, width=width, hidden=hidden),
        out_shape=[back] * count + [dval] * count,
        in_specs=[pl.BlockSpec(memory_space=pltpu.SMEM)] + [vmem] * (count + 2),
        out_specs=[vmem] * (2 * count),
        cost_estimate=pl.CostEstimate(
            flops=flops, transcendentals=2 * count * rows * hidden, bytes_accessed=12 * width * hidden
        ),
        name="experts%d" % count,
    )(ids, *msgs, own, neighbour)
    return out[:count], out[count:]


def outer_kernel(start_ref, *refs, count, hidden, add):
    xs = refs[:count]
    dys = refs[count : 2 * count]
    dvals = refs[2 * count : 3 * count]
    out = refs[-1]
    join = lambda parts, lo, hi: jnp.concatenate([r[:, lo:hi] for r in parts], axis=0)
    tile = xs[0].shape[1]
    x = join(xs, 0, tile)
    dy = join(dys, 0, tile)
    pair = lax.dot_general(x, join(dvals, 0, 2 * hidden), ROWS_T, preferred_element_type=F32)
    down = lax.dot_general(dy, join(dvals, 2 * hidden, 3 * hidden), ROWS_T, preferred_element_type=F32)
    for k, value in enumerate((pair[:, :hidden], pair[:, hidden:], down)):
        if add:
            value = value + refs[3 * count][k].astype(F32)
        out[k] = value.astype(out.dtype)


def outer(start, msgs, dvals, which, width, hidden, half_rows, dtype, more=None):
    count = len(msgs)
    rows = msgs[0].shape[0]
    tile = 2 * LANES
    shift = width // tile
    in_specs = [pl.BlockSpec((rows, tile), lambda t, s: (0, s[0] + t))] * count
    in_specs += [pl.BlockSpec((rows, tile), lambda t, s: (0, shift + s[0] + t))] * count
    in_specs += [pl.BlockSpec((rows, 3 * hidden), lambda t, s: (0, which))] * count
    args = list(msgs) + list(msgs) + list(dvals)
    if more is not None:
        in_specs.append(pl.BlockSpec((3, tile, hidden), lambda t, s: (0, t, 0)))
        args.append(more)
    return pl.pallas_call(
        functools.partial(outer_kernel, count=count, hidden=hidden, add=more is not None),
        out_shape=jax.ShapeDtypeStruct((3, half_rows, hidden), dtype),
        grid_spec=pltpu.PrefetchScalarGridSpec(
            num_scalar_prefetch=1,
            grid=(half_rows // tile,),
            in_specs=in_specs,
            out_specs=pl.BlockSpec((3, tile, hidden), lambda t, s: (0, t, 0)),
        ),
        cost_estimate=pl.CostEstimate(
            flops=6 * count * rows * half_rows * hidden,
            transcendentals=0,
            bytes_accessed=4 * count * rows * half_rows + 6 * half_rows * hidden,
        ),
        name="outer%d" % which,
    )(start, *args)


def folded_line(n):
    return [0] + list(range(1, n, 2)) + [k for k in range(n - 1, 0, -1) if k % 2 == 0]


def dense_body(tokens, grad_out, expert_ids, route_weight, experts, error_in, hot_expert, keep_rows):
    n_owners = lax.axis_size("ep")
    n_cores = lax.axis_size("dp")
    tok_count, _ = expert_ids.shape
    width = tokens.shape[1]
    hidden = experts.shape[3]
    half_rows = width // n_cores
    me = lax.axis_index("ep").astype(jnp.int32)
    core = lax.axis_index("dp").astype(jnp.int32)
    row_start = core * half_rows
    hot_id = hot_expert[0]
    n_line = n_owners // 4
    order = folded_line(n_line)
    after = {order[k]: order[(k + 1) % n_line] for k in range(n_line)}
    across = lambda v, bit: lax.ppermute(v, "ep", [(i, i ^ bit) for i in range(n_owners)])
    along = lambda v: lax.ppermute(
        v, "ep", [(4 * z + q, 4 * after[z] + q) for z in range(n_line) for q in range(4)]
    )
    swap = lambda v: lax.ppermute(v, "dp", [(0, 1), (1, 0)])
    two_of = lambda mine, theirs, axis: jnp.where(
        core == 0,
        jnp.concatenate([mine, theirs], axis=axis),
        jnp.concatenate([theirs, mine], axis=axis),
    )

    owned = experts[0]
    lanes = -(-n_owners // LANES) * LANES
    named = expert_ids[:, :, None] == jnp.arange(lanes, dtype=jnp.int32)[None, None, :]
    probs = jnp.sum(jnp.where(named, route_weight[:, :, None], 0).astype(F32), axis=1).astype(BF16)
    message = jnp.concatenate([tokens, grad_out, probs], axis=1)
    near_part = across(lax.dynamic_slice_in_dim(owned, row_start, half_rows, 1), 1)
    column = [message]
    for _ in range(n_line - 1):
        column.append(along(column[-1]))
    other = [across(m, 2) for m in column]
    near = two_of(near_part, swap(near_part), 1)
    ids = jnp.stack([me, me ^ 1, hot_id])

    backs, dvals = {}, {}
    rounds = [(("c", k), ("o", k)) for k in range(n_line - 1)] + [(("c", n_line - 1),), (("o", n_line - 1),)]
    all_msgs = {("c", k): column[k] for k in range(n_line)} | {("o", k): other[k] for k in range(n_line)}
    for keys in rounds:
        got_back, got_dval = run_experts(ids, [all_msgs[k] for k in keys], owned, near)
        for k, b, d in zip(keys, got_back, got_dval):
            backs[k], dvals[k] = b, d
    keys = [k for one in rounds for k in one]
    msgs = [all_msgs[k] for k in keys]
    dvs = [dvals[k] for k in keys]

    tiles = half_rows // (2 * LANES)
    mine_at = (core * tiles).reshape(1)
    theirs_at = ((1 - core) * tiles).reshape(1)
    grad = functools.partial(outer, msgs=msgs, dvals=dvs, width=width, hidden=hidden, half_rows=half_rows)
    near_sib = swap(grad(theirs_at, which=1, dtype=BF16))
    own_sib = swap(grad(theirs_at, which=0, dtype=BF16))
    near_sum = grad(mine_at, which=1, dtype=BF16, more=near_sib)
    own_near = across(near_sum, 1)
    own_sum = grad(mine_at, which=0, dtype=F32, more=own_sib)

    wide = lambda v: v.astype(F32)
    here = lambda k: wide(backs["c", k]) + wide(across(backs["o", k], 2))
    part = None
    for k in range(1, n_line):
        part = here(k) if part is None else wide(along(part)) + here(k)
        part = part.astype(BF16)
    final = here(0) if part is None else wide(along(part)) + here(0)
    d_tokens = final[:, :width].astype(BF16)
    score = final[:, width : width + lanes]
    d_route = jnp.sum(jnp.where(named, score[:, None, :], 0.0), axis=2).astype(BF16)
    d_hot = final[:, width + lanes :].astype(BF16)

    cut = lambda v, c: lax.dynamic_slice_in_dim(v, c * half_rows, half_rows, 1)
    both = lambda c: jnp.concatenate([cut(tokens, c), cut(grad_out, c)], axis=1)
    rows2 = jnp.concatenate([both(core), swap(both(1 - core))], axis=0)
    hot2 = jnp.concatenate([d_hot, swap(d_hot)], axis=0)
    from_x = lax.dot_general(
        rows2[:, :half_rows], hot2[:, : 2 * hidden], ROWS_T, preferred_element_type=F32
    )
    from_dy = lax.dot_general(
        rows2[:, half_rows:], hot2[:, 2 * hidden :], ROWS_T, preferred_element_type=F32
    )
    shadow = jnp.stack([from_x[:, :hidden], from_x[:, hidden:], from_dy])
    accum = shadow + wide(error_in[0])
    hits = (keep_rows - row_start)[:, None] == jnp.arange(half_rows, dtype=jnp.int32)[None, :]
    dropped = jnp.any(hits, axis=0)
    error_out = jnp.where(dropped[None, :, None], 0.0, accum).astype(BF16)[None]

    kept_count = keep_rows.shape[0]
    kept_half = kept_count // n_cores
    kept = jnp.einsum("kr,crf->kcf", hits.astype(BF16), error_in[0], preferred_element_type=F32)
    part_of = lambda c: lax.dynamic_slice_in_dim(kept, c * kept_half, kept_half, 0)
    kept = part_of(core) + swap(part_of(1 - core))
    kept = kept + across(kept, 1)
    kept = kept + across(kept, 2)
    moving = kept
    for _ in range(n_line - 1):
        moving = along(moving)
        kept = kept + moving
    kept = two_of(kept, swap(kept), 0).reshape(kept_count, 3 * hidden)
    spread_kept = lax.dot_general(
        hits.astype(F32), kept, ROWS_T, precision=lax.Precision.HIGHEST, preferred_element_type=F32
    )
    spread_kept = jnp.stack([spread_kept[:, k * hidden : (k + 1) * hidden] for k in range(3)])
    total = own_sum + wide(own_near)
    hot_total = jnp.where(dropped[None, :, None], total + spread_kept, 0.0)
    d_experts = jnp.where(me == hot_id, hot_total, total).astype(BF16)[None]
    return (d_tokens, d_route, d_experts, error_out)


def body(*args):
    n_owners = lax.axis_size("ep")
    top_count = args[2].shape[1]
    dense = n_owners % 4 == 0 and lax.axis_size("dp") == 2 and n_owners <= 2 * top_count
    return dense_body(*args) if dense else sparse_body(*args)


def solution(mesh):
    in_specs = (
        P(("ep", "dp"), None),
        P(("ep", "dp"), None),
        P(("ep", "dp"), None),
        P(("ep", "dp"), None),
        P("ep", None, None, None),
        P("ep", None, "dp", None),
        P(),
        P(),
    )
    out_specs = (
        P(("ep", "dp"), None),
        P(("ep", "dp"), None),
        P("ep", None, "dp", None),
        P("ep", None, "dp", None),
    )
    return jax.shard_map(body, mesh=mesh, in_specs=in_specs, out_specs=out_specs, check_vma=False)
```

```python
import functools
import jax
import jax.numpy as jnp
from jax import lax
from jax.experimental import pallas as pl
from jax.experimental.pallas import tpu as pltpu
from jax.sharding import PartitionSpec as P


def spread(x, axis, root):
    mine = lax.axis_index(axis) == root
    return lax.psum(jnp.where(mine, x, jnp.zeros_like(x)), axis)


def expert_rows(rows_x, rows_dy, rows_p, weights):
    gate_pre = jnp.dot(rows_x, weights[0], preferred_element_type=jnp.float32)
    up_pre = jnp.dot(rows_x, weights[1], preferred_element_type=jnp.float32)
    back_proj = jnp.dot(rows_dy, weights[2], preferred_element_type=jnp.float32)
    sigmoid_g = jax.nn.sigmoid(gate_pre)
    silu_g = gate_pre * sigmoid_g
    active = silu_g * up_pre
    d_score = jnp.sum(active * back_proj, axis=1).astype(jnp.bfloat16)
    scale_p = rows_p.astype(jnp.float32)[:, None]
    grad_h = scale_p * back_proj
    d_gate = (grad_h * up_pre * sigmoid_g * (1.0 + gate_pre * (1.0 - sigmoid_g))).astype(
        jnp.bfloat16
    )
    d_up = (grad_h * silu_g).astype(jnp.bfloat16)
    hidden_w = (scale_p * active).astype(jnp.bfloat16)
    contract = (((1,), (1,)), ((), ()))
    grad_x = (
        lax.dot_general(d_gate, weights[0], contract, preferred_element_type=jnp.float32)
        + lax.dot_general(d_up, weights[1], contract, preferred_element_type=jnp.float32)
    ).astype(jnp.bfloat16)
    outer = (((0,), (0,)), ((), ()))
    grads = jnp.stack(
        [
            lax.dot_general(rows_x, d_gate, outer, preferred_element_type=jnp.float32),
            lax.dot_general(rows_x, d_up, outer, preferred_element_type=jnp.float32),
            lax.dot_general(rows_dy, hidden_w, outer, preferred_element_type=jnp.float32),
        ]
    )
    return (grad_x, d_score, grads)


def sparse_body(tokens, grad_out, expert_ids, route_weight, experts, error_in, hot_expert, keep_rows):
    n_owners = lax.axis_size("ep")
    n_cores = lax.axis_size("dp")
    tok_count, top_count = expert_ids.shape
    width = tokens.shape[1]
    assigns = tok_count * top_count
    capacity = 9 * assigns // (8 * n_owners)
    slot_rows = n_owners * capacity
    half_rows = width // n_cores
    row_start = lax.axis_index("dp") * half_rows
    hot_id = hot_expert[0]
    flat_ids = expert_ids.reshape(assigns)
    position = jnp.arange(assigns, dtype=jnp.int32)
    onehot = (flat_ids[:, None] == jnp.arange(n_owners, dtype=jnp.int32)[None, :]).astype(
        jnp.bfloat16
    )
    earlier = (position[:, None] > position[None, :]).astype(jnp.bfloat16)
    before = jnp.dot(earlier, onehot, preferred_element_type=jnp.float32)
    ranks = jnp.sum(before * onehot.astype(jnp.float32), axis=1).astype(jnp.int32)
    slot_of = flat_ids * capacity + ranks
    source = jnp.full((slot_rows,), -1, jnp.int32).at[slot_of].set(position)
    filled = source >= 0
    safe_idx = jnp.maximum(source, 0)
    owner_row = jnp.arange(slot_rows, dtype=jnp.int32) // capacity
    cold_slot = filled & (owner_row != hot_id)
    slot_x = jnp.where(filled[:, None], jnp.take(tokens, safe_idx // top_count, axis=0), 0)
    slot_dy = jnp.where(filled[:, None], jnp.take(grad_out, safe_idx // top_count, axis=0), 0)
    slot_p = jnp.where(filled, jnp.take(route_weight.reshape(assigns), safe_idx), 0)
    send_x = jnp.where(cold_slot[:, None], slot_x, 0).reshape(n_owners, capacity, width)
    send_dy = jnp.where(cold_slot[:, None], slot_dy, 0).reshape(n_owners, capacity, width)
    send_p = jnp.where(cold_slot, slot_p, 0).reshape(n_owners, capacity)
    recv_x, recv_dy, recv_p = (
        lax.all_to_all(send_x, "ep", split_axis=0, concat_axis=0, tiled=True),
        lax.all_to_all(send_dy, "ep", split_axis=0, concat_axis=0, tiled=True),
        lax.all_to_all(send_p, "ep", split_axis=0, concat_axis=0, tiled=True),
    )
    owned = experts[0]
    my_rows = lax.dynamic_slice_in_dim(owned, row_start, half_rows, 1)
    hot_rows = spread(my_rows, "ep", hot_id)
    hot_weights = lax.all_gather(hot_rows, "dp", axis=1, tiled=True)
    cold_dx, cold_score, cold_grads = expert_rows(
        recv_x.reshape(slot_rows, width),
        recv_dy.reshape(slot_rows, width),
        recv_p.reshape(slot_rows),
        owned,
    )
    back_dx, back_score = (
        lax.all_to_all(
            cold_dx.reshape(n_owners, capacity, width),
            "ep",
            split_axis=0,
            concat_axis=0,
            tiled=True,
        ),
        lax.all_to_all(
            cold_score.reshape(n_owners, capacity), "ep", split_axis=0, concat_axis=0, tiled=True
        ),
    )
    hot_x = lax.dynamic_slice_in_dim(slot_x, hot_id * capacity, capacity, 0)
    hot_dy = lax.dynamic_slice_in_dim(slot_dy, hot_id * capacity, capacity, 0)
    hot_p = lax.dynamic_slice_in_dim(slot_p, hot_id * capacity, capacity, 0)
    hot_dx, hot_score, hot_grads = expert_rows(hot_x, hot_dy, hot_p, hot_weights)
    all_dx = lax.dynamic_update_slice_in_dim(
        back_dx.reshape(slot_rows, width), hot_dx, hot_id * capacity, 0
    )
    all_score = lax.dynamic_update_slice_in_dim(
        back_score.reshape(slot_rows), hot_score, hot_id * capacity, 0
    )
    d_tokens = jnp.sum(
        jnp.take(all_dx, slot_of, axis=0).astype(jnp.float32).reshape(tok_count, top_count, width),
        axis=1,
    ).astype(jnp.bfloat16)
    d_route = jnp.take(all_score, slot_of).reshape(tok_count, top_count)
    cold_sum, shadow_sum = (
        lax.psum_scatter(
            cold_grads.astype(jnp.bfloat16), "dp", scatter_dimension=1, tiled=True
        ).astype(jnp.float32),
        lax.psum_scatter(
            hot_grads.astype(jnp.bfloat16), "dp", scatter_dimension=1, tiled=True
        ).astype(jnp.float32),
    )
    accum = shadow_sum + error_in[0].astype(jnp.float32)
    local_keep = keep_rows - row_start
    inside = (local_keep >= 0) & (local_keep < half_rows)
    clipped = jnp.clip(local_keep, 0, half_rows - 1)
    chosen = jnp.where(inside[None, :, None], jnp.take(accum, clipped, axis=1), 0.0)
    dropped = jnp.zeros((half_rows,), jnp.int32).at[clipped].add(inside.astype(jnp.int32)) > 0
    error_out = jnp.where(dropped[None, :, None], 0.0, accum).astype(jnp.bfloat16)[None]
    kept = lax.psum(chosen, "ep")
    unpacked = (
        jnp.zeros_like(accum).at[:, clipped, :].add(jnp.where(inside[None, :, None], kept, 0.0))
    )
    is_owner = lax.axis_index("ep") == hot_id
    d_experts = (cold_sum + jnp.where(is_owner, unpacked, 0.0)).astype(jnp.bfloat16)[None]
    return (d_tokens, d_route, d_experts, error_out)


LANES = 128
TILE = 4 * LANES
SLAB = 16
EXPERT_VMEM = 16 << 20
OUTER_VMEM = 16 << 20
BF16 = jnp.bfloat16
F32 = jnp.float32
ROWS_T = (((0,), (0,)), ((), ()))
COLS_T = (((1,), (1,)), ((), ()))


def expert_kernel(ids_ref, *refs, count, blocks, width, hidden):
    msgs = refs[:count]
    own, near_lo, near_hi = refs[count : count + 3]
    backs = refs[count + 3 : count + 3 + blocks]
    dvals = refs[count + 3 + blocks : count + 3 + 2 * blocks]
    buffer, pre, sems = refs[count + 3 + 2 * blocks :]
    tok = buffer.shape[0] // blocks
    half = near_lo.shape[1]
    offsets = [0]
    for m in msgs:
        offsets.append(offsets[-1] + m.shape[0])
    cols = buffer.shape[1]
    cuts = (slice(0, width), slice(width, cols))
    copies = [
        [
            pltpu.make_async_copy(
                msgs[i].at[:, cuts[k]],
                buffer.at[pl.ds(offsets[i], msgs[i].shape[0]), cuts[k]],
                sems.at[k, i],
            )
            for i in range(count)
        ]
        for k in range(2)
    ]
    for part in copies:
        for copy in part:
            copy.start()
    for copy in copies[0]:
        copy.wait()
    x = buffer[:, :width]
    own_dot = lambda v, k: jnp.dot(v, own[k], preferred_element_type=F32)
    near_dot = lambda v, k: jnp.dot(v[:, :half], near_lo[k], preferred_element_type=F32) + jnp.dot(
        v[:, half:], near_hi[k], preferred_element_type=F32
    )

    def pre_step(k, _):
        for n, dot in enumerate((own_dot, near_dot)):
            pre[n, k] = dot(x, k)
        return 0

    lax.fori_loop(0, 2, pre_step, 0)
    for copy in copies[1]:
        copy.wait()
    dy = buffer[:, width : 2 * width]
    probs = buffer[:, 2 * width :].astype(F32)
    lane = lax.broadcasted_iota(jnp.int32, probs.shape, 1)
    score = jnp.zeros(probs.shape, F32)
    hot = ids_ref[2]
    pair = []
    for n, dot in enumerate((own_dot, near_dot)):
        mine = lane == ids_ref[n]
        p = jnp.sum(jnp.where(mine, probs, 0.0), axis=1, keepdims=True)
        gate, up = pre[n, 0], pre[n, 1]
        back = dot(dy, 2)
        sig = jax.nn.sigmoid(gate)
        silu = gate * sig
        act = silu * up
        score = jnp.where(mine, jnp.sum(act * back, axis=1, keepdims=True), score)
        grad_h = p * back
        d_gate = (grad_h * up * sig * (1.0 + gate * (1.0 - sig))).astype(BF16)
        d_up = (grad_h * silu).astype(BF16)
        hidden_w = (p * act).astype(BF16)
        pair.append((d_gate, d_up, hidden_w))
        for i in range(blocks):
            for k, d in enumerate((d_gate, d_up, hidden_w)):
                lo = (3 * n + k) * hidden
                dvals[i][:, lo : lo + hidden] = d[i * tok : (i + 1) * tok]
    columns = (width - tok) // hidden
    p_hot = jnp.sum(jnp.where(lane == hot, probs, 0.0), axis=1, keepdims=True)
    row = lax.broadcasted_iota(jnp.int32, (tok, tok), 0)
    col = lax.broadcasted_iota(jnp.int32, (tok, tok), 1)
    earlier = (row > col).astype(BF16)
    for i in range(blocks):
        held = jnp.broadcast_to((p_hot[i * tok : (i + 1) * tok] > 0.0).astype(F32), (tok, tok))
        rank = jnp.dot(earlier, held.astype(BF16), preferred_element_type=F32).astype(jnp.int32)
        pick = jnp.where(rank == col, held, 0.0).astype(BF16)
        backs[i][tok:, :] = jnp.zeros((backs[i].shape[0] - tok, width), BF16)
        for n in range(2):

            @pl.when(hot == ids_ref[n])
            def _():
                for k in range(3):
                    lo = (3 * n + k) * hidden
                    packed = lax.dot_general(
                        pick, dvals[i][:, lo : lo + hidden], ROWS_T, preferred_element_type=F32
                    ).astype(BF16)
                    for c in range(columns):
                        backs[i][tok + k * SLAB : tok + (k + 1) * SLAB, c * hidden : (c + 1) * hidden] = (
                            packed[c * SLAB : (c + 1) * SLAB]
                        )

        flipped = jnp.transpose(score[i * tok : (i + 1) * tok])[:SLAB].astype(BF16)
        backs[i][tok : tok + SLAB, width - tok :] = flipped

    d_all = jnp.concatenate([pair[0][0], pair[0][1], pair[1][0], pair[1][1]], axis=1)
    step = 2 * LANES

    def dx_step(t, _):
        at = pl.multiple_of(t * step, step)
        for near, to in ((near_lo, at), (near_hi, pl.multiple_of(half + at, step))):
            part = jnp.concatenate(
                [own[k, pl.ds(to, step), :] for k in range(2)] + [near[k, pl.ds(at, step), :] for k in range(2)],
                axis=1,
            )
            dx = lax.dot_general(d_all, part, COLS_T, preferred_element_type=F32).astype(BF16)
            for i in range(blocks):
                backs[i][:tok, pl.ds(to, step)] = dx[i * tok : (i + 1) * tok]
        return 0

    lax.fori_loop(0, half // step, dx_step, 0)


def run_experts(ids, msgs, own, near, tok):
    count = len(msgs)
    cols = msgs[0].shape[1]
    _, width, hidden = own.shape
    vmem = pl.BlockSpec(memory_space=pltpu.VMEM)
    rows = sum(m.shape[0] for m in msgs)
    blocks = rows // tok
    back = [jax.ShapeDtypeStruct((tok + 3 * SLAB, width), BF16)] * blocks
    dval = [jax.ShapeDtypeStruct((tok, 6 * hidden), BF16)] * blocks
    flops = 20 * rows * width * hidden
    out = pl.pallas_call(
        functools.partial(expert_kernel, count=count, blocks=blocks, width=width, hidden=hidden),
        out_shape=back + dval,
        in_specs=[pl.BlockSpec(memory_space=pltpu.SMEM)]
        + [pl.BlockSpec(memory_space=pl.ANY)] * count
        + [vmem] * 3,
        out_specs=[vmem] * (2 * blocks),
        scratch_shapes=[
            pltpu.VMEM((rows, cols), BF16),
            pltpu.VMEM((2, 2, rows, hidden), F32),
            pltpu.SemaphoreType.DMA((2, count)),
        ],
        cost_estimate=pl.CostEstimate(
            flops=flops, transcendentals=2 * rows * hidden, bytes_accessed=12 * width * hidden
        ),
        compiler_params=pltpu.CompilerParams(vmem_limit_bytes=EXPERT_VMEM),
    )(ids, *msgs, own, *near)
    return out[:blocks], out[blocks:]


def outer_kernel(ids_ref, *refs, count, blocks, hidden):
    xs = refs[:count]
    dys = refs[count : 2 * count]
    dvals = refs[2 * count : 2 * count + blocks]
    more = refs[2 * count + blocks : -2]
    outs = refs[-2:]
    join = lambda parts, at, size: jnp.concatenate([r[:, pl.ds(at, size)] for r in parts], axis=0)
    step = 2 * LANES

    def part(t, _):
        at = pl.multiple_of(t * step, step)
        pair_d = jnp.concatenate([join(dvals, 3 * n * hidden, 2 * hidden) for n in range(2)], axis=1)
        down_d = jnp.concatenate([join(dvals, (3 * n + 2) * hidden, hidden) for n in range(2)], axis=1)
        pair = lax.dot_general(join(xs, at, step), pair_d, ROWS_T, preferred_element_type=F32)
        down = lax.dot_general(join(dys, at, step), down_d, ROWS_T, preferred_element_type=F32)
        for n, out in enumerate(outs):
            parts = [pair[:, (2 * n + k) * hidden : (2 * n + k + 1) * hidden] for k in range(2)]
            for k, value in enumerate(parts + [down[:, n * hidden : (n + 1) * hidden]]):
                if more and n == 1:
                    value = value + more[0][k, pl.ds(at, step), :].astype(F32)
                out[k, pl.ds(at, step), :] = value.astype(out.dtype)
        return 0

    lax.fori_loop(0, xs[0].shape[1] // step, part, 0)


def outer(ids, which, more, msgs, dvals, width, hidden, half_rows):
    count = len(msgs)
    rows = [m.shape[0] for m in msgs]
    tile = TILE
    shift = width // tile
    vmem = pl.BlockSpec(memory_space=pltpu.VMEM)
    square = pl.BlockSpec((3, tile, hidden), lambda t, s: (0, t, 0))
    in_specs = [pl.BlockSpec((r, tile), lambda t, s: (0, s[which] + t)) for r in rows]
    in_specs += [pl.BlockSpec((r, tile), lambda t, s: (0, shift + s[which] + t)) for r in rows]
    return pl.pallas_call(
        functools.partial(outer_kernel, count=count, blocks=len(dvals), hidden=hidden),
        out_shape=[jax.ShapeDtypeStruct((3, half_rows, hidden), BF16)] * 2,
        grid_spec=pltpu.PrefetchScalarGridSpec(
            num_scalar_prefetch=1,
            grid=(half_rows // tile,),
            in_specs=in_specs + [vmem] * len(dvals) + [square] * len(more),
            out_specs=[square] * 2,
        ),
        cost_estimate=pl.CostEstimate(
            flops=12 * sum(rows) * half_rows * hidden,
            transcendentals=0,
            bytes_accessed=4 * sum(rows) * half_rows + 12 * half_rows * hidden,
        ),
        compiler_params=pltpu.CompilerParams(vmem_limit_bytes=OUTER_VMEM),
        name="outer",
    )(ids, *msgs, *msgs, *dvals, *more)


def spread_kernel(hits, rows, out):
    parts, count, hidden = out.shape

    def part(t, _):
        at = pl.multiple_of(t * LANES, LANES)
        value = lax.dot_general(hits[:, pl.ds(at, LANES)], rows[...], ROWS_T, preferred_element_type=F32)
        for k in range(parts):
            out[k, pl.ds(at, LANES), :] = value[:, k * hidden : (k + 1) * hidden]
        return 0

    lax.fori_loop(0, count // LANES, part, 0)


def spread_rows(hits, rows, hidden):
    vmem = pl.BlockSpec(memory_space=pltpu.VMEM)
    return pl.pallas_call(
        spread_kernel,
        out_shape=jax.ShapeDtypeStruct((rows.shape[1] // hidden, hits.shape[1], hidden), F32),
        in_specs=[vmem, vmem],
        out_specs=vmem,
        compiler_params=pltpu.CompilerParams(vmem_limit_bytes=OUTER_VMEM),
        name="spread",
    )(hits, rows)


def folded_line(n):
    return [0] + list(range(1, n, 2)) + [k for k in range(n - 1, 0, -1) if k % 2 == 0]


def dense_body(tokens, grad_out, expert_ids, route_weight, experts, error_in, hot_expert, keep_rows):
    n_owners = lax.axis_size("ep")
    n_cores = lax.axis_size("dp")
    tok_count, _ = expert_ids.shape
    width = tokens.shape[1]
    hidden = experts.shape[3]
    half_rows = width // n_cores
    me = lax.axis_index("ep").astype(jnp.int32)
    core = lax.axis_index("dp").astype(jnp.int32)
    row_start = core * half_rows
    hot_id = hot_expert[0]
    n_line = n_owners // 4
    order = folded_line(n_line)
    after = {order[k]: order[(k + 1) % n_line] for k in range(n_line)}
    across = lambda v, bit: lax.ppermute(v, "ep", [(i, i ^ bit) for i in range(n_owners)])
    along = lambda v: lax.ppermute(
        v, "ep", [(4 * z + q, 4 * after[z] + q) for z in range(n_line) for q in range(4)]
    )
    swap = lambda v: lax.ppermute(v, "dp", [(0, 1), (1, 0)])
    owned = experts[0]
    lanes = -(-n_owners // LANES) * LANES
    last = n_line - 1
    split = tok_count // 2
    named = expert_ids[:, :, None] == jnp.arange(lanes, dtype=jnp.int32)[None, None, :]
    probs = jnp.sum(jnp.where(named, route_weight[:, :, None], 0).astype(F32), axis=1).astype(BF16)
    message = jnp.concatenate([tokens, grad_out, probs], axis=1)
    kept_count = keep_rows.shape[0]
    kept_half = kept_count // n_cores
    tiles = half_rows // TILE
    ids = jnp.stack([me, me ^ 1, hot_id, core * tiles, (1 - core) * tiles])
    scalars = (core == 0, me == hot_id, row_start, half_rows - row_start, core * kept_half, kept_half - core * kept_half)
    message, ids, scalars = lax.optimization_barrier((message, ids, scalars))
    first_core, owns_hot, row_start, other_start, kept_start, kept_other = scalars

    def cut(v, start, size, axis):
        at = [jnp.int32(0)] * v.ndim
        at[axis] = start
        sizes = list(v.shape)
        sizes[axis] = size
        return lax.dynamic_slice(v, at, sizes, allow_negative_indices=False)

    two_of = lambda mine, theirs, axis: jnp.where(
        first_core,
        jnp.concatenate([mine, theirs], axis=axis),
        jnp.concatenate([theirs, mine], axis=axis),
    )
    column, other = [message], []
    for k in range(n_line):
        other.append(across(column[k][:split] if k == last else column[k], 2))
        if k < last:
            column.append(along(column[k]))
    late = along(other[last - 1][split:])
    near_part = across(cut(owned, row_start, half_rows, 1), 1)
    near_rest = swap(near_part)
    near = (jnp.where(first_core, near_part, near_rest), jnp.where(first_core, near_rest, near_part))

    backs, all_msgs = {}, {}
    all_msgs["o", last] = (other[last], late)
    msgs, dvs = [], []
    for k in [1, 0] + list(range(2, n_line)):
        pieces = [column[k], *(all_msgs["o", k] if k == last else [other[k]])]
        got_back, got_dval = run_experts(ids, pieces, owned, near, tok_count)
        backs["c", k], backs["o", k] = got_back
        msgs += pieces
        dvs += got_dval

    grad = functools.partial(outer, msgs=msgs, dvals=dvs, width=width, hidden=hidden, half_rows=half_rows)
    wide = lambda v: v.astype(F32)
    own_sib, near_sib = grad(ids, 4, ())
    near_sib = swap(near_sib)
    own_sib = swap(own_sib)
    own_sum, near_sum = grad(ids, 3, (near_sib,))
    own_near = across(near_sum, 1)

    def home(value):
        return wide(across(value, 2))

    def onward(value):
        return wide(along(value))

    part = None
    for k in range(1, last):
        here = wide(backs["c", k]) + home(backs["o", k])
        part = (here if part is None else onward(part) + here).astype(BF16)
    far = backs["o", last]
    cut_at = far.shape[0] // (2 * SLAB) * SLAB + SLAB
    near_home = home(far[:cut_at])
    near_home = jnp.pad(near_home, ((0, far.shape[0] - cut_at), (0, 0)))
    part = (onward(part) + wide(backs["c", last]) + near_home).astype(BF16)
    side = wide(along(far[cut_at:]))
    side = (wide(backs["o", 0]) + jnp.pad(side, ((cut_at, 0), (0, 0)))).astype(BF16)
    final = onward(part) + wide(backs["c", 0]) + home(side)
    d_tokens = final[:tok_count].astype(BF16)
    slabs = final[tok_count:]
    score = slabs[:SLAB, width - tok_count :].T[:, None, :]
    d_route = jnp.sum(jnp.where(named[:, :, :SLAB], score, 0.0), axis=2).astype(BF16)
    slots = (width - tok_count) // hidden * SLAB
    packed = slabs.astype(BF16)
    slab = lambda k, c: packed[k * SLAB : (k + 1) * SLAB, c * hidden : (c + 1) * hidden]
    d_hot = jnp.concatenate(
        [jnp.concatenate([slab(k, c) for c in range(slots // SLAB)], axis=0) for k in range(3)], axis=1
    )

    wants = jnp.any(expert_ids == hot_id, axis=1)
    before = jnp.arange(tok_count)[:, None] > jnp.arange(tok_count)[None, :]
    rank = jnp.sum(jnp.where(before & wants[None, :], 1, 0), axis=1)
    pick = (rank[None, :] == jnp.arange(slots)[:, None]) & wants[None, :]
    hot_rows = jnp.dot(
        pick.astype(BF16), message[:, : 2 * width], preferred_element_type=F32
    ).astype(BF16)
    both = lambda start: jnp.concatenate(
        [cut(hot_rows[:, lo : lo + width], start, half_rows, 1) for lo in (0, width)], axis=1
    )
    rows2 = jnp.concatenate([both(row_start), swap(both(other_start))], axis=0)
    hot2 = jnp.concatenate([d_hot, swap(d_hot)], axis=0)
    from_x = lax.dot_general(
        rows2[:, :half_rows], hot2[:, : 2 * hidden], ROWS_T, preferred_element_type=F32
    )
    from_dy = lax.dot_general(
        rows2[:, half_rows:], hot2[:, 2 * hidden :], ROWS_T, preferred_element_type=F32
    )
    shadow = jnp.stack([from_x[:, :hidden], from_x[:, hidden:], from_dy])
    accum = shadow + wide(error_in[0])
    hits = (keep_rows - row_start)[:, None] == jnp.arange(half_rows, dtype=jnp.int32)[None, :]
    dropped = jnp.any(hits, axis=0)
    error_out = jnp.where(dropped[None, :, None], 0.0, accum).astype(BF16)[None]

    kept = jnp.einsum("kr,crf->kcf", hits.astype(BF16), error_in[0], preferred_element_type=F32)
    kept = cut(kept, kept_start, kept_half, 0) + wide(swap(cut(kept, kept_other, kept_half, 0).astype(BF16)))
    kept = kept + wide(across(kept.astype(BF16), 1))
    bit = 4
    while bit < n_owners:
        kept = kept + wide(across(kept.astype(BF16), bit))
        bit *= 2
    kept = kept + wide(across(kept.astype(BF16), 2))
    kept = two_of(kept, swap(kept), 0).reshape(kept_count, 3 * hidden)
    high = lax.reduce_precision(kept, 8, 7)
    two_parts = jnp.concatenate([high, kept - high], axis=0).astype(BF16)
    hits2 = jnp.concatenate([hits, hits], axis=0).astype(BF16)
    spread_kept = spread_rows(hits2, two_parts, hidden)
    whole = wide(own_sum) + wide(own_sib)
    unsent = owns_hot & ~dropped[None, :, None]
    base = jnp.where(owns_hot, jnp.where(unsent, 0.0, whole + spread_kept), whole)
    base = lax.optimization_barrier(base)
    d_experts = (base + jnp.where(unsent, 0.0, wide(own_near))).astype(BF16)[None]
    return (d_tokens, d_route, d_experts, error_out)


def body(*args):
    n_owners = lax.axis_size("ep")
    top_count = args[2].shape[1]
    dense = n_owners == 2 * top_count == SLAB and lax.axis_size("dp") == 2
    if not dense:
        return sparse_body(*args)
    return dense_body(*args)


def solution(mesh):
    in_specs = (
        P(("ep", "dp"), None),
        P(("ep", "dp"), None),
        P(("ep", "dp"), None),
        P(("ep", "dp"), None),
        P("ep", None, None, None),
        P("ep", None, "dp", None),
        P(),
        P(),
    )
    out_specs = (
        P(("ep", "dp"), None),
        P(("ep", "dp"), None),
        P("ep", None, "dp", None),
        P("ep", None, "dp", None),
    )
    return jax.shard_map(body, mesh=mesh, in_specs=in_specs, out_specs=out_specs, check_vma=False)
```
